32 devices in a mesh: section: 2 (over core), dp: 4 (over y, x), tensor: 4 (over z).
Axes of the slice: x: 2, y: 2, z: 4, core: 2. Of those that a mesh axis runs over, the one named last changes fastest.
Arguments:
- boundary: float32 [2, 12, 256, 2048], P('section', 'dp', 'tensor'), may hold values from -24 to 24
- segments: int32 [12, 256], P('dp'), may hold values from 0 to 3, never falling along the last dimension, each value on 1 to 128 neighbouring positions
- w_qkv: bfloat16 [2, 2048, 3, 2048], P('section', 'dp', None, 'tensor'), may hold values from -0.125 to 0.125
- w_out: bfloat16 [2, 2048, 2048], P('section', 'tensor', 'dp'), may hold values from -0.125 to 0.125
- w_gate_up: bfloat16 [2, 2048, 2, 8192], P('section', 'dp', None, 'tensor'), may hold values from -0.125 to 0.125
- w_down: bfloat16 [2, 8192, 2048], P('section', 'tensor', 'dp'), may hold values from -0.0625 to 0.0625
- gains: bfloat16 [2, 4, 2048], P('section', None, 'dp'), may hold values from 0.5 to 2
Outputs:
- section_out: float32 [2, 12, 256, 2048], P('section', 'dp', 'tensor')
- section_grad: float32 [2, 12, 256, 2048], P('section', 'dp', 'tensor')
- grad_qkv: float32 [2, 2048, 3, 2048], P('section', 'dp', None, 'tensor')
- grad_attn_out: float32 [2, 2048, 2048], P('section', 'tensor', 'dp')
- grad_gate_up: float32 [2, 2048, 2, 8192], P('section', 'dp', None, 'tensor')
- grad_down: float32 [2, 8192, 2048], P('section', 'tensor', 'dp')
- grad_gains: float32 [2, 4, 2048], P('section', None, 'dp')
The draws below stay inside these ranges and needn't reach their ends.
Inputs may be any that keep to these rules, and one draw needn't show every extreme that they name: `segments`: segment ids never fall along a sequence; each of the 4 documents of a sequence covers 1 to 128 positions.
All inputs are finite; a program needn't handle non-finite values.
Results may differ from the reference program's by a relative error of at most 0.035.
Values may be sent and summed in bfloat16 or wider, within the bound.
No kernel may reach another device: no remote copies, remote signals or barrier semaphores. Data moves between devices by JAX's collectives and lax.ppermute only.
A program may use at most 384 MiB of HBM per device.

```python
import math
import jax
import jax.numpy as jnp
import numpy as np
from jax import lax

D = 2048
HEADS = 16
HD = 128
FF = 8192
SEQ = 256
SEQ_MB = 1
MICRO = 3
DOCS = 4
DOC_MOST = 128
SEQS = 12


def draw_boundary(key, part):
    key_base = jax.random.fold_in(key, 0)
    normal_part = jax.random.normal(key_base, (2, SEQS, SEQ, D), jnp.float32)
    return jnp.clip(normal_part, -24.0, 24.0)


def draw_gains(key, part):
    key_base = jax.random.fold_in(key, 0)
    return jnp.exp(jax.random.uniform(key_base, (2, 4, D), jnp.float32, math.log(0.5), math.log(2.0))).astype(jnp.bfloat16)


def levels(rng, dims, shards, smallest, high):
    level = 1.0
    for axis_at, parts in shards:
        heights = jax.random.uniform(jax.random.fold_in(jax.random.fold_in(rng, 6), axis_at), (parts,), jnp.float32, smallest / len(shards), high / len(shards))
        level = level * jnp.repeat(jnp.exp(heights), dims[axis_at] // parts).reshape((-1,) + (1,) * (len(dims) - 1 - axis_at))
    return level


def split_up(count, total, limit, skew):
    weights = [(1 << 20) // math.isqrt(rank ** skew) + 1 for rank in range(2, count + 1)]
    rest, given = total - limit - (count - 1), [1] * (count - 1)
    while rest > 0:
        candidates = [i for i in range(count - 1) if given[i] < limit]
        whole, left = sum([weights[i] for i in candidates]), rest
        for i in candidates:
            extra = min(limit - given[i], max(1, left * weights[i] // whole), rest)
            given[i] = given[i] + extra
            rest = rest - extra
    return np.array([limit] + given)


def ragged_sizes(rng, count, total, limit, slope):
    if count == 2:
        one = jax.random.randint(rng, (), max(1, total - limit), min(limit, total - 1) + 1)
        return jnp.stack([one, total - one])
    tallies = jnp.asarray(split_up(count, total, limit, slope), jnp.int32)
    twos = (count - 1) // 2
    giver, taker = tallies[1:1 + 2 * twos:2], tallies[2:2 + 2 * twos:2]
    margin = jnp.minimum(giver - 1, limit - taker)
    shifted = jax.random.randint(jax.random.fold_in(rng, 1), (twos,), 0, 1 << 20) % (margin + 1)
    tallies = tallies.at[1:1 + 2 * twos:2].set(giver - shifted).at[2:2 + 2 * twos:2].set(taker + shifted)
    return tallies[jax.random.permutation(jax.random.fold_in(rng, 2), count)]


def noise(rng, shape, width, reach, shards=(), held_as=jnp.bfloat16):
    array = width * jax.random.normal(rng, shape, jnp.float32)
    if shards:
        array = array * levels(rng, shape, shards, -0.22, 0.18)
    return jnp.clip(array, -reach, reach).astype(held_as)


def setup_inputs(seed: int = 0) -> dict:
    seeds = jax.random.split(jax.random.key(seed), 8)
    boundary = draw_boundary(jax.random.fold_in(seeds[7], 71), 0)
    segments = jax.vmap(lambda own: jnp.searchsorted(jnp.cumsum(ragged_sizes(own, DOCS, SEQ, DOC_MOST, 2)), jnp.arange(SEQ), side="right"))(jax.random.split(seeds[1], SEQS)).reshape((SEQS, SEQ)).astype(jnp.int32)
    w_qkv = noise(seeds[2], (2, D, 3, D), D ** -0.5, 0.125, ((0, 2), (1, 4), (3, 4)))
    w_out = noise(seeds[3], (2, D, D), D ** -0.5, 0.125, ((0, 2), (1, 4), (2, 4)))
    w_gate_up = noise(seeds[4], (2, D, 2, FF), D ** -0.5, 0.125, ((0, 2), (1, 4), (3, 4)))
    w_down = noise(seeds[5], (2, FF, D), FF ** -0.5, 0.0625, ((0, 2), (1, 4), (2, 4)))
    gains = draw_gains(jax.random.fold_in(seeds[7], 71), 0)
    return dict(boundary=boundary, segments=segments, w_qkv=w_qkv, w_out=w_out, w_gate_up=w_gate_up, w_down=w_down, gains=gains)


EPS = 1e-06
THETA = 500000.0

def matmul(left, right):
    return jnp.dot(left, right, preferred_element_type=jnp.float32)

def rms_scale(vectors):
    return lax.rsqrt(lax.optimization_barrier(jnp.mean(vectors * vectors, axis=-1, keepdims=True)) + EPS)

def segment_tables(seg_rows):
    same_doc = seg_rows[:, :, None] == seg_rows[:, None, :]
    index_row = jnp.arange(seg_rows.shape[1], dtype=jnp.int32)
    earlier = index_row[None, :] < index_row[:, None]
    positions = lax.optimization_barrier(jnp.sum((same_doc & earlier[None]).astype(jnp.int32), axis=-1))
    visible = same_doc & (index_row[None, :] <= index_row[:, None])[None]
    half_dim = HD // 2
    inverse_freq = THETA ** (-(jnp.arange(half_dim, dtype=jnp.float32) * (2.0 / HD)))
    angles = positions.astype(jnp.float32)[..., None] * inverse_freq
    return (visible, jnp.cos(angles), jnp.sin(angles))

def rotate(vectors, cosine, sine_part):
    half_dim = HD // 2
    front_half = vectors[..., :half_dim]
    back_half = vectors[..., half_dim:]
    cos_wide = cosine[:, :, None, :]
    sin_wide = sine_part[:, :, None, :]
    return jnp.concatenate([front_half * cos_wide - back_half * sin_wide, back_half * cos_wide + front_half * sin_wide], axis=-1)

def masked_scores(query_rot, key_rot, visible):
    scores = jnp.einsum('bshe,bthe->bhst', query_rot.astype(jnp.float32), key_rot.astype(jnp.float32)) * HD ** (-0.5)
    return jnp.where(visible[:, None], scores, -jnp.inf)

def log_norm(masked):
    row_max = lax.optimization_barrier(jnp.max(masked, axis=-1, keepdims=True))
    return row_max + jnp.log(lax.optimization_barrier(jnp.sum(jnp.exp(masked - row_max), axis=-1, keepdims=True)))

def layer_forward(layer_in, visible, cosine, sine_part, w_attn, w_mix, w_ffn, w_back, norm_gains):
    seq_count = layer_in.shape[0]
    tokens = seq_count * SEQ
    layer_in_bf = layer_in.astype(jnp.bfloat16).reshape(tokens, D)
    proj_qkv = matmul(layer_in_bf, w_attn.reshape(D, 3 * D)).reshape(seq_count, SEQ, 3, D)
    queries = proj_qkv[:, :, 0]
    key_vecs = proj_qkv[:, :, 1]
    values = proj_qkv[:, :, 2].astype(jnp.bfloat16)
    query_scale = rms_scale(queries)
    key_scale = rms_scale(key_vecs)
    query_hat = queries * query_scale
    key_hat = key_vecs * key_scale
    query_rot = rotate((query_hat * norm_gains[0]).reshape(seq_count, SEQ, HEADS, HD), cosine, sine_part).astype(jnp.bfloat16)
    key_rot = rotate((key_hat * norm_gains[1]).reshape(seq_count, SEQ, HEADS, HD), cosine, sine_part).astype(jnp.bfloat16)
    masked = masked_scores(query_rot, key_rot, visible)
    log_total = log_norm(masked)
    attn_probs = jnp.exp(masked - log_total)
    value_heads = values.reshape(seq_count, SEQ, HEADS, HD)
    attn_mix = jnp.einsum('bhst,bthe->bshe', attn_probs.astype(jnp.bfloat16).astype(jnp.float32), value_heads.astype(jnp.float32))
    attn_mix = attn_mix.astype(jnp.bfloat16).reshape(tokens, D)
    attn_proj = matmul(attn_mix, w_mix).reshape(seq_count, SEQ, D)
    attn_scale = rms_scale(attn_proj)
    attn_hat = attn_proj * attn_scale
    hidden = layer_in + attn_hat * norm_gains[2]
    hidden_bf = hidden.astype(jnp.bfloat16).reshape(tokens, D)
    gate_up = matmul(hidden_bf, w_ffn.reshape(D, 2 * FF)).reshape(tokens, 2, FF)
    gate_pre = gate_up[:, 0]
    up_pre = gate_up[:, 1]
    swiglu = (jax.nn.silu(gate_pre) * up_pre).astype(jnp.bfloat16)
    ffn_proj = matmul(swiglu, w_back).reshape(seq_count, SEQ, D)
    ffn_scale = rms_scale(ffn_proj)
    ffn_hat = ffn_proj * ffn_scale
    output = hidden + ffn_hat * norm_gains[3]
    kept_arrays = (layer_in_bf, query_hat, key_hat, query_scale, key_scale, query_rot, key_rot, value_heads, log_total, attn_mix, attn_hat, attn_scale, hidden_bf, gate_pre, up_pre, swiglu, ffn_hat, ffn_scale)
    return (output, kept_arrays)

def layer_backward(back_output, kept_arrays, visible, cosine, sine_part, w_attn, w_mix, w_ffn, w_back, norm_gains):
    layer_in_bf, query_hat, key_hat, query_scale, key_scale, query_rot, key_rot, value_heads, log_total, attn_mix, attn_hat, attn_scale, hidden_bf, gate_pre, up_pre, swiglu, ffn_hat, ffn_scale = kept_arrays
    seq_count = back_output.shape[0]
    tokens = seq_count * SEQ
    gain_ffn = lax.optimization_barrier(jnp.sum(back_output * ffn_hat, axis=(0, 1)))
    back_ffn_hat = back_output * norm_gains[3]
    back_ffn = ffn_scale * (back_ffn_hat - ffn_hat * lax.optimization_barrier(jnp.mean(back_ffn_hat * ffn_hat, axis=-1, keepdims=True)))
    back_ffn_bf = back_ffn.astype(jnp.bfloat16).reshape(tokens, D)
    grad_down_part = matmul(swiglu.T, back_ffn_bf)
    back_swiglu = matmul(back_ffn_bf, w_back.T)
    sigmoid_gate = jax.nn.sigmoid(gate_pre)
    back_gate = (back_swiglu * up_pre * sigmoid_gate * (1.0 + gate_pre * (1.0 - sigmoid_gate))).astype(jnp.bfloat16)
    back_up = (back_swiglu * jax.nn.silu(gate_pre)).astype(jnp.bfloat16)
    back_gate_up = jnp.concatenate([back_gate, back_up], axis=1)
    ffn_flat = w_ffn.reshape(D, 2 * FF)
    grad_ffn_part = matmul(hidden_bf.T, back_gate_up).reshape(D, 2, FF)
    back_hidden = back_output + matmul(back_gate_up, ffn_flat.T).reshape(seq_count, SEQ, D)
    gain_attn = lax.optimization_barrier(jnp.sum(back_hidden * attn_hat, axis=(0, 1)))
    back_attn_hat = back_hidden * norm_gains[2]
    back_attn = attn_scale * (back_attn_hat - attn_hat * lax.optimization_barrier(jnp.mean(back_attn_hat * attn_hat, axis=-1, keepdims=True)))
    back_attn_bf = back_attn.astype(jnp.bfloat16).reshape(tokens, D)
    grad_mix_part = matmul(attn_mix.T, back_attn_bf)
    back_mix = matmul(back_attn_bf, w_mix.T).astype(jnp.bfloat16).reshape(seq_count, SEQ, HEADS, HD)
    masked = masked_scores(query_rot, key_rot, visible)
    attn_probs = jnp.exp(masked - log_total)
    probs_bf = attn_probs.astype(jnp.bfloat16)
    back_values = jnp.einsum('bhst,bshe->bthe', probs_bf.astype(jnp.float32), back_mix.astype(jnp.float32)).astype(jnp.bfloat16)
    back_probs = jnp.einsum('bshe,bthe->bhst', back_mix.astype(jnp.float32), value_heads.astype(jnp.float32))
    row_dot = lax.optimization_barrier(jnp.sum(attn_probs * back_probs, axis=-1, keepdims=True))
    back_scores = (attn_probs * (back_probs - row_dot) * HD ** (-0.5)).astype(jnp.bfloat16)
    back_query_rot = jnp.einsum('bhst,bthe->bshe', back_scores.astype(jnp.float32), key_rot.astype(jnp.float32))
    back_key_rot = jnp.einsum('bhst,bshe->bthe', back_scores.astype(jnp.float32), query_rot.astype(jnp.float32))
    back_query_gained = rotate(back_query_rot, cosine, -sine_part).reshape(seq_count, SEQ, D)
    back_key_gained = rotate(back_key_rot, cosine, -sine_part).reshape(seq_count, SEQ, D)
    gain_query = lax.optimization_barrier(jnp.sum(back_query_gained * query_hat, axis=(0, 1)))
    gain_key = lax.optimization_barrier(jnp.sum(back_key_gained * key_hat, axis=(0, 1)))
    back_query_hat = back_query_gained * norm_gains[0]
    back_key_hat = back_key_gained * norm_gains[1]
    back_query = (query_scale * (back_query_hat - query_hat * lax.optimization_barrier(jnp.mean(back_query_hat * query_hat, axis=-1, keepdims=True)))).astype(jnp.bfloat16)
    back_key = (key_scale * (back_key_hat - key_hat * lax.optimization_barrier(jnp.mean(back_key_hat * key_hat, axis=-1, keepdims=True)))).astype(jnp.bfloat16)
    back_qkv = jnp.stack([back_query, back_key, back_values.reshape(seq_count, SEQ, D)], axis=2).reshape(tokens, 3 * D)
    grad_attn_part = matmul(layer_in_bf.T, back_qkv).reshape(D, 3, D)
    back_input = back_hidden + matmul(back_qkv, w_attn.reshape(D, 3 * D).T).reshape(seq_count, SEQ, D)
    gain_part = jnp.stack([gain_query, gain_key, gain_attn, gain_ffn])
    return (back_input, (grad_attn_part, grad_mix_part, grad_ffn_part, grad_down_part, gain_part))

def reference(boundary, segments, w_qkv, w_out, w_gate_up, w_down, gains):
    seq_block = SEQ_MB * MICRO
    num_blocks = SEQS // seq_block
    inputs = boundary[0].reshape(num_blocks, seq_block, SEQ, D)
    cotangents = boundary[1].reshape(num_blocks, seq_block, SEQ, D)
    seg_blocks = segments.reshape(num_blocks, seq_block, SEQ)
    first_layer = (w_qkv[0], w_out[0], w_gate_up[0], w_down[0], gains[0])
    second_layer = (w_qkv[1], w_out[1], w_gate_up[1], w_down[1], gains[1])

    def block_step(totals, block_data):
        first_in, last_cotangent, seg_rows = block_data
        visible, cosine, sine_part = segment_tables(seg_rows)
        first_out, first_kept = layer_forward(first_in, visible, cosine, sine_part, *first_layer)
        second_out, second_kept = layer_forward(first_out, visible, cosine, sine_part, *second_layer)
        second_back, second_grads = layer_backward(last_cotangent, second_kept, visible, cosine, sine_part, *second_layer)
        first_back, first_grads = layer_backward(second_back, first_kept, visible, cosine, sine_part, *first_layer)
        totals = jax.tree.map(lambda total, early, late: total + jnp.stack([early, late]), totals, first_grads, second_grads)
        return (totals, (first_out, second_out, first_back, second_back))
    zero_grads = (jnp.zeros((2, D, 3, D), jnp.float32), jnp.zeros((2, D, D), jnp.float32), jnp.zeros((2, D, 2, FF), jnp.float32), jnp.zeros((2, FF, D), jnp.float32), jnp.zeros((2, 4, D), jnp.float32))
    totals, (first_out, second_out, first_back, second_back) = lax.scan(block_step, zero_grads, (inputs, cotangents, seg_blocks))
    section_out = jnp.stack([first_out.reshape(SEQS, SEQ, D), second_out.reshape(SEQS, SEQ, D)])
    section_grad = jnp.stack([first_back.reshape(SEQS, SEQ, D), second_back.reshape(SEQS, SEQ, D)])
    return (section_out, section_grad, totals[0], totals[1], totals[2], totals[3], totals[4])
```

```python
import jax
import jax.numpy as jnp
from jax import lax
from jax.sharding import PartitionSpec as P

D = 2048
HD = 128
MICRO = 3


EPS = 1e-06
THETA = 500000.0

GROUPS = ((0, 1, 2),)


def matmul(left, right):
    return jnp.dot(left, right, preferred_element_type=jnp.float32)


def inner_left(left, right):
    return lax.dot_general(
        left, right, (((0,), (0,)), ((), ())), preferred_element_type=jnp.float32
    )


def inner_right(left, right):
    return lax.dot_general(
        left, right, (((1,), (1,)), ((), ())), preferred_element_type=jnp.float32
    )


def rms_scale(vectors):
    return lax.rsqrt(jnp.mean(vectors * vectors, axis=-1, keepdims=True) + EPS)


def swap_cores(block):
    return lax.ppermute(block, "section", [(0, 1), (1, 0)])


def one_way(block, source):
    return lax.ppermute(block, "section", [(source, 1 - source)])


def from_ahead(block, distance):
    size = lax.axis_size("tensor")
    return lax.ppermute(block, "tensor", [(i, (i - distance) % size) for i in range(size)])


def to_ahead(block, distance):
    size = lax.axis_size("tensor")
    return lax.ppermute(block, "tensor", [(i, (i + distance) % size) for i in range(size)])


def gather_tokens(rows):
    size = lax.axis_size("tensor")
    mine = jnp.stack([rows] + [from_ahead(rows, j) for j in range(1, size)], axis=1)
    other = swap_cores(mine)
    return jnp.concatenate([mine, other], axis=1)


def scatter_tokens(partial):
    size = lax.axis_size("tensor")
    other = swap_cores(partial[:, size:].astype(jnp.bfloat16))
    chip = partial[:, :size] + other.astype(jnp.float32)
    total = chip[:, 0]
    sent = chip.astype(jnp.bfloat16)
    for j in range(1, size):
        total = total + to_ahead(sent[:, j], j).astype(jnp.float32)
    return total


def sum_heads(parts, seqs):
    size = lax.axis_size("tensor")
    split = parts.reshape(parts.shape[0], seqs, 2, size, -1)
    chip = split + swap_cores(split)[:, :, ::-1]
    total = chip
    for j in range(1, size):
        total = total + jnp.roll(from_ahead(chip, j), j, axis=3)
    return total.reshape(parts.shape)


def local_order(table, section_index, tensor_rank):
    seqs, length = table.shape
    size = lax.axis_size("tensor")
    split = table.reshape(seqs, size, 2, length // (2 * size))
    twice = jnp.concatenate([split, split], axis=1)
    turned = lax.dynamic_slice_in_dim(twice, tensor_rank, size, 1)
    turned = jnp.where(section_index == 0, turned, turned[:, :, ::-1])
    return jnp.transpose(turned, (0, 2, 1, 3)).reshape(seqs, length)


def doc_tables(seg_rows, section_index, tensor_rank):
    same_doc = seg_rows[:, :, None] == seg_rows[:, None, :]
    index_row = jnp.arange(seg_rows.shape[1], dtype=jnp.int32)
    earlier = index_row[None, :] < index_row[:, None]
    positions = jnp.sum((same_doc & earlier[None]).astype(jnp.int32), axis=-1)
    positions = local_order(positions, section_index, tensor_rank)
    segs = local_order(seg_rows, section_index, tensor_rank)
    order = local_order(
        jnp.broadcast_to(index_row[None], seg_rows.shape), section_index, tensor_rank
    )
    visible = (segs[:, :, None] == segs[:, None, :]) & (order[:, None, :] <= order[:, :, None])
    half_dim = HD // 2
    inverse_freq = THETA ** (-(jnp.arange(half_dim, dtype=jnp.float32) * (2.0 / HD)))
    angles = positions.astype(jnp.float32)[..., None] * inverse_freq
    return (visible, jnp.cos(angles), jnp.sin(angles))


def rotate(vectors, cosine, sine_part):
    half_dim = HD // 2
    front_half = vectors[..., :half_dim]
    back_half = vectors[..., half_dim:]
    cos_wide = cosine[:, :, None, :]
    sin_wide = sine_part[:, :, None, :]
    return jnp.concatenate(
        [
            front_half * cos_wide - back_half * sin_wide,
            back_half * cos_wide + front_half * sin_wide,
        ],
        axis=-1,
    )


def masked_scores(query_rot, key_rot, visible):
    scores = jnp.einsum(
        "bshe,bthe->bhst", query_rot, key_rot, preferred_element_type=jnp.float32
    ) * HD ** (-0.5)
    return jnp.where(visible[:, None], scores, -jnp.inf)


def log_norm(masked):
    row_max = jnp.max(masked, axis=-1, keepdims=True)
    return row_max + jnp.log(jnp.sum(jnp.exp(masked - row_max), axis=-1, keepdims=True))


class Layer:
    def __init__(self, w_qkv, w_out, w_gate_up, w_down, gains, head_slot):
        self.w_qkv = w_qkv
        self.w_out = w_out
        self.w_gate_up = w_gate_up
        self.w_down = w_down
        self.gains = gains
        width = w_out.shape[0]
        self.query_gain = lax.dynamic_slice_in_dim(gains[0], head_slot * width, width)
        self.key_gain = lax.dynamic_slice_in_dim(gains[1], head_slot * width, width)
        self.head_slot = head_slot

    def attend(self, layer_in, tables):
        visible, cosine, sine_part = tables
        full = gather_tokens(layer_in.astype(jnp.bfloat16))
        seqs, slots, rows, _ = full.shape
        length = slots * rows
        tokens = seqs * length
        full = full.reshape(tokens, D)
        width = self.w_out.shape[0]
        heads = width // HD
        qkv = matmul(full, self.w_qkv)
        queries = qkv[:, :width]
        key_vecs = qkv[:, width : 2 * width]
        values = qkv[:, 2 * width :].astype(jnp.bfloat16).reshape(seqs, length, heads, HD)
        squares = sum_heads(
            jnp.stack([jnp.sum(queries * queries, axis=-1), jnp.sum(key_vecs * key_vecs, axis=-1)]),
            seqs,
        )
        scales = lax.rsqrt(squares / D + EPS)
        query_scale = scales[0][:, None]
        key_scale = scales[1][:, None]
        query_hat = queries * query_scale
        key_hat = key_vecs * key_scale
        query_rot = rotate(
            (query_hat * self.query_gain).reshape(seqs, length, heads, HD), cosine, sine_part
        ).astype(jnp.bfloat16)
        key_rot = rotate(
            (key_hat * self.key_gain).reshape(seqs, length, heads, HD), cosine, sine_part
        ).astype(jnp.bfloat16)
        masked = masked_scores(query_rot, key_rot, visible)
        log_total = log_norm(masked)
        probs = jnp.exp(masked - log_total)
        mix = jnp.einsum(
            "bhst,bthe->bshe",
            probs.astype(jnp.bfloat16),
            values,
            preferred_element_type=jnp.float32,
        )
        mix = mix.astype(jnp.bfloat16).reshape(tokens, width)
        attn = scatter_tokens(matmul(mix, self.w_out).reshape(seqs, slots, rows, D))
        attn_scale = rms_scale(attn)
        attn_hat = attn * attn_scale
        hidden = layer_in + attn_hat * self.gains[2]
        kept = dict(
            full=full,
            query_hat=query_hat,
            key_hat=key_hat,
            query_scale=query_scale,
            key_scale=key_scale,
            query_rot=query_rot,
            key_rot=key_rot,
            values=values,
            log_total=log_total,
            mix=mix,
            attn_hat=attn_hat,
            attn_scale=attn_scale,
            tables=tables,
        )
        return hidden, kept

    def feed(self, hidden, kept):
        full = gather_tokens(hidden.astype(jnp.bfloat16))
        seqs, slots, rows, _ = full.shape
        full = full.reshape(seqs * slots * rows, D)
        units = self.w_down.shape[0]
        gate_up = matmul(full, self.w_gate_up)
        gate = gate_up[:, :units]
        up = gate_up[:, units:]
        swiglu = (jax.nn.silu(gate) * up).astype(jnp.bfloat16)
        ffn = scatter_tokens(matmul(swiglu, self.w_down).reshape(seqs, slots, rows, D))
        ffn_scale = rms_scale(ffn)
        ffn_hat = ffn * ffn_scale
        output = hidden + ffn_hat * self.gains[3]
        kept = dict(
            kept,
            full_hidden=full,
            gate=gate,
            up=up,
            swiglu=swiglu,
            ffn_hat=ffn_hat,
            ffn_scale=ffn_scale,
        )
        return output, kept

    def feed_back(self, back_output, kept):
        ffn_hat = kept["ffn_hat"]
        gain_ffn = jnp.sum(back_output * ffn_hat, axis=(0, 1))
        back_hat = back_output * self.gains[3]
        back_ffn = kept["ffn_scale"] * (
            back_hat - ffn_hat * jnp.mean(back_hat * ffn_hat, axis=-1, keepdims=True)
        )
        full = gather_tokens(back_ffn.astype(jnp.bfloat16))
        shape = full.shape
        full = full.reshape(-1, D)
        grad_down = inner_left(kept["swiglu"], full)
        back_swiglu = inner_right(full, self.w_down)
        gate = kept["gate"]
        up = kept["up"]
        sigmoid_gate = jax.nn.sigmoid(gate)
        back_gate = back_swiglu * up * sigmoid_gate * (1.0 + gate * (1.0 - sigmoid_gate))
        back_up = back_swiglu * jax.nn.silu(gate)
        back_gate_up = jnp.concatenate([back_gate, back_up], axis=1).astype(jnp.bfloat16)
        back_hidden = back_output + scatter_tokens(
            inner_right(back_gate_up, self.w_gate_up).reshape(shape)
        )
        grad_gate_up = inner_left(kept["full_hidden"], back_gate_up)
        return back_hidden, dict(down=grad_down, gate_up=grad_gate_up, gain_ffn=gain_ffn)

    def attend_back(self, back_hidden, kept, grads):
        visible, cosine, sine_part = kept["tables"]
        attn_hat = kept["attn_hat"]
        gain_attn = jnp.sum(back_hidden * attn_hat, axis=(0, 1))
        back_hat = back_hidden * self.gains[2]
        back_attn = kept["attn_scale"] * (
            back_hat - attn_hat * jnp.mean(back_hat * attn_hat, axis=-1, keepdims=True)
        )
        full = gather_tokens(back_attn.astype(jnp.bfloat16))
        shape = full.shape
        full = full.reshape(-1, D)
        tokens = full.shape[0]
        query_rot = kept["query_rot"]
        key_rot = kept["key_rot"]
        values = kept["values"]
        heads_shape = values.shape
        grad_out = inner_left(kept["mix"], full)
        back_mix = inner_right(full, self.w_out).astype(jnp.bfloat16).reshape(heads_shape)
        masked = masked_scores(query_rot, key_rot, visible)
        probs = jnp.exp(masked - kept["log_total"])
        back_values = jnp.einsum(
            "bhst,bshe->bthe",
            probs.astype(jnp.bfloat16),
            back_mix,
            preferred_element_type=jnp.float32,
        ).astype(jnp.bfloat16)
        back_probs = jnp.einsum(
            "bshe,bthe->bhst", back_mix, values, preferred_element_type=jnp.float32
        )
        row_dot = jnp.sum(probs * back_probs, axis=-1, keepdims=True)
        back_scores = (probs * (back_probs - row_dot) * HD ** (-0.5)).astype(jnp.bfloat16)
        back_query_rot = jnp.einsum(
            "bhst,bthe->bshe", back_scores, key_rot, preferred_element_type=jnp.float32
        )
        back_key_rot = jnp.einsum(
            "bhst,bshe->bthe", back_scores, query_rot, preferred_element_type=jnp.float32
        )
        width = self.w_out.shape[0]
        back_query_gained = rotate(back_query_rot, cosine, -sine_part).reshape(tokens, width)
        back_key_gained = rotate(back_key_rot, cosine, -sine_part).reshape(tokens, width)
        query_hat = kept["query_hat"]
        key_hat = kept["key_hat"]
        gain_query = jnp.sum(back_query_gained * query_hat, axis=0)
        gain_key = jnp.sum(back_key_gained * key_hat, axis=0)
        back_query_hat = back_query_gained * self.query_gain
        back_key_hat = back_key_gained * self.key_gain
        dots = sum_heads(
            jnp.stack(
                [
                    jnp.sum(back_query_hat * query_hat, axis=-1),
                    jnp.sum(back_key_hat * key_hat, axis=-1),
                ]
            ),
            shape[0],
        )
        back_query = kept["query_scale"] * (back_query_hat - query_hat * (dots[0] / D)[:, None])
        back_key = kept["key_scale"] * (back_key_hat - key_hat * (dots[1] / D)[:, None])
        back_qkv = jnp.concatenate(
            [
                back_query.astype(jnp.bfloat16),
                back_key.astype(jnp.bfloat16),
                back_values.reshape(tokens, width),
            ],
            axis=1,
        )
        back_input = back_hidden + scatter_tokens(
            inner_right(back_qkv, self.w_qkv).reshape(shape)
        )
        grad_qkv = inner_left(kept["full"], back_qkv)
        zero_width = jnp.zeros((D,), jnp.float32)
        start = self.head_slot * width
        gain_part = jnp.stack(
            [
                lax.dynamic_update_slice(zero_width, gain_query, (start,)),
                lax.dynamic_update_slice(zero_width, gain_key, (start,)),
                gain_attn,
                grads["gain_ffn"],
            ]
        )
        grads = dict(
            out=grad_out,
            qkv=grad_qkv,
            gains=gain_part,
            down=grads["down"],
            gate_up=grads["gate_up"],
        )
        return back_input, grads


def body(boundary, segments, w_qkv, w_out, w_gate_up, w_down, gains):
    section_index = lax.axis_index("section")
    tensor_rank = lax.axis_index("tensor")
    first = section_index == 0

    def shared(block, axis):
        half = block.shape[axis] // 2
        kept = lax.dynamic_slice_in_dim(block, section_index * half, half, axis)
        sent = lax.dynamic_slice_in_dim(block, (1 - section_index) * half, half, axis)
        received = swap_cores(sent)
        return jnp.where(first, kept, received), jnp.where(first, received, kept)

    rows_in, rows_back = shared(boundary[0], 1)
    model = w_qkv.shape[1]
    qkv_halves = [half.reshape(model, -1) for half in shared(w_qkv[0], 2)]
    out_halves = shared(w_out[0], 0)
    gate_up_halves = [half.reshape(model, -1) for half in shared(w_gate_up[0], 2)]
    down_halves = shared(w_down[0], 0)
    other_gains = swap_cores(gains[0])
    both_gains = jnp.stack(
        [jnp.where(first, gains[0], other_gains), jnp.where(first, other_gains, gains[0])]
    )
    all_gains = lax.all_gather(both_gains, "dp", axis=2, tiled=True)
    head_slot = tensor_rank * 2 + section_index
    layers = []
    for index in range(2):
        layers.append(
            Layer(
                lax.all_gather(qkv_halves[index], "dp", axis=0, tiled=True),
                lax.all_gather(out_halves[index], "dp", axis=1, tiled=True),
                lax.all_gather(gate_up_halves[index], "dp", axis=0, tiled=True),
                lax.all_gather(down_halves[index], "dp", axis=1, tiled=True),
                all_gains[index],
                head_slot,
            )
        )
    tables = doc_tables(segments, section_index, tensor_rank)
    states = []
    for group in GROUPS:
        low, high = group[0], group[-1] + 1
        states.append(
            dict(
                rows=rows_in[low:high],
                back=rows_back[low:high],
                tables=tuple(table[low:high] for table in tables),
                kept=[],
                outs=[],
                backs=[],
            )
        )
    for layer in layers:
        for state in states:
            state["hidden"], state["now"] = layer.attend(state["rows"], state["tables"])
        for state in states:
            state["rows"], kept = layer.feed(state["hidden"], state["now"])
            state["kept"].append(kept)
            state["outs"].append(state["rows"])
    all_grads = []
    for index in (1, 0):
        layer = layers[index]
        totals = None
        for state in states:
            state["hidden"], state["grads"] = layer.feed_back(state["back"], state["kept"][index])
        for state in states:
            state["back"], grads = layer.attend_back(
                state["hidden"], state["kept"][index], state["grads"]
            )
            state["backs"].append(state["back"])
            totals = grads if totals is None else jax.tree.map(jnp.add, totals, grads)

        def summed(name, axis):
            return lax.psum_scatter(
                totals[name].astype(jnp.bfloat16), "dp", scatter_dimension=axis, tiled=True
            )

        all_grads.append(
            dict(
                down=summed("down", 1),
                gate_up=summed("gate_up", 0),
                out=summed("out", 1),
                qkv=summed("qkv", 0),
                gains=lax.psum_scatter(
                    lax.psum(totals["gains"], ("section", "tensor")),
                    "dp",
                    scatter_dimension=1,
                    tiled=True,
                ),
            )
        )
    second_grads, first_grads = all_grads

    def collected(name, axis, shape):
        mine_first = first_grads[name].reshape(shape)
        mine_second = second_grads[name].reshape(shape)
        to_second = one_way(mine_second, 0)
        to_first = one_way(mine_first, 1)
        low = jnp.where(first, mine_first, to_second)
        high = jnp.where(first, to_first, mine_second)
        return jnp.concatenate([low, high], axis=axis).astype(jnp.float32)[None]

    def placed(first_rows, second_rows):
        to_second = one_way(second_rows, 0)
        to_first = one_way(first_rows, 1)
        low = jnp.where(first, first_rows, to_second)
        high = jnp.where(first, to_first, second_rows)
        return jnp.concatenate([low, high], axis=1)[None]

    outs = [jnp.concatenate([state["outs"][i] for state in states], axis=0) for i in range(2)]
    backs = [jnp.concatenate([state["backs"][i] for state in states], axis=0) for i in range(2)]
    units = w_down.shape[1] // 2
    width = w_out.shape[1] // 2
    return (
        placed(outs[0], outs[1]),
        placed(backs[1], backs[0]),
        collected("qkv", 2, (model, 3, width)),
        collected("out", 0, (width, w_out.shape[2])),
        collected("gate_up", 2, (model, 2, units)),
        collected("down", 0, (units, w_down.shape[2])),
        jnp.where(first, first_grads["gains"], second_grads["gains"])[None],
    )


def solution(mesh):
    return jax.shard_map(
        body,
        mesh=mesh,
        in_specs=(
            P("section", "dp", "tensor", None),
            P("dp", None),
            P("section", "dp", None, "tensor"),
            P("section", "tensor", "dp"),
            P("section", "dp", None, "tensor"),
            P("section", "tensor", "dp"),
            P("section", None, "dp"),
        ),
        out_specs=(
            P("section", "dp", "tensor", None),
            P("section", "dp", "tensor", None),
            P("section", "dp", None, "tensor"),
            P("section", "tensor", "dp"),
            P("section", "dp", None, "tensor"),
            P("section", "tensor", "dp"),
            P("section", None, "dp"),
        ),
        check_vma=False,
    )
```

```python
import jax
import jax.numpy as jnp
from jax import lax
from jax.sharding import PartitionSpec as P


D = 2048
HD = 128


EPS = 1e-06
THETA = 500000.0


def matmul(left, right):
    return jnp.dot(left, right, preferred_element_type=jnp.float32)


def inner_left(left, right):
    return lax.dot_general(
        left, right, (((0,), (0,)), ((), ())), preferred_element_type=jnp.float32
    )


def inner_right(left, right):
    return lax.dot_general(
        left, right, (((1,), (1,)), ((), ())), preferred_element_type=jnp.float32
    )


def rms_scale(vectors):
    return lax.rsqrt(jnp.mean(vectors * vectors, axis=-1, keepdims=True) + EPS)


def swap_cores(block):
    return lax.ppermute(block, "section", [(0, 1), (1, 0)])


def one_way(block, source):
    return lax.ppermute(block, "section", [(source, 1 - source)])


def from_ahead(block, distance):
    size = lax.axis_size("tensor")
    return lax.ppermute(block, "tensor", [(i, (i - distance) % size) for i in range(size)])


def to_ahead(block, distance):
    size = lax.axis_size("tensor")
    return lax.ppermute(block, "tensor", [(i, (i + distance) % size) for i in range(size)])


def square():
    return lax.axis_size("dp") == 4


def across(block, flip):
    return lax.ppermute(block, "dp", [(i, i ^ flip) for i in range(4)])


def local_blocks(array):
    if not square():
        return array
    rank = lax.axis_index("dp")
    width = array.shape[-1] // 4
    return jnp.concatenate(
        [
            lax.dynamic_slice_in_dim(array, (rank ^ j) * width, width, array.ndim - 1)
            for j in range(4)
        ],
        axis=-1,
    )


def gather_blocks(block):
    if not square():
        return list(lax.all_gather(block, "dp", axis=0, tiled=False))
    half = block.shape[0] // 2
    by_x = across(block, 1)
    by_y = across(block, 2)
    low = across(by_y[:half], 1)
    high = across(by_x[half:], 2)
    return [block, by_x, by_y, jnp.concatenate([low, high], axis=0)]


def scatter_blocks(blocks):
    wire = jnp.bfloat16
    if not square():
        whole = jnp.concatenate([block.astype(wire) for block in blocks], axis=0)
        return lax.psum_scatter(whole, "dp", scatter_dimension=0, tiled=True).astype(jnp.float32)
    half = blocks[0].shape[0] // 2
    own, to_x, to_y, to_far = [block.astype(wire) for block in blocks]
    by_x = across(jnp.concatenate([to_far[:half], to_x[:half]], axis=0), 1)
    by_y = across(jnp.concatenate([to_far[half:], to_y[half:]], axis=0), 2)

    def added(left, right):
        return left.astype(jnp.float32) + right.astype(jnp.float32)

    high = across(added(to_x[half:], by_y[:half]).astype(wire), 1)
    low = across(added(to_y[:half], by_x[:half]).astype(wire), 2)
    by_x, by_y, low, high = lax.optimization_barrier((by_x, by_y, low, high))
    low = added(own[:half], by_x[half:]) + low.astype(jnp.float32)
    high = added(own[half:], by_y[half:]) + high.astype(jnp.float32)
    return jnp.concatenate([low, high], axis=0)


def split_last(array):
    return jnp.split(array, lax.axis_size("dp"), axis=-1)


def split_first(array):
    return jnp.split(array, lax.axis_size("dp"), axis=0)


def gather_tokens(rows):
    size = lax.axis_size("tensor")
    slots = [rows]
    for j in range(1, size):
        slots.append(from_ahead(rows, j))
    mine = jnp.stack(slots, axis=1)
    other = swap_cores(mine)
    return jnp.concatenate([mine, other], axis=1)


def scatter_tokens(partial):
    size = lax.axis_size("tensor")
    other = swap_cores(partial[:, size:].astype(jnp.bfloat16))
    chip = partial[:, :size] + other.astype(jnp.float32)
    total = chip[:, 0]
    sent = chip.astype(jnp.bfloat16)
    for j in range(1, size):
        total = total + to_ahead(sent[:, j], j).astype(jnp.float32)
    return total


def sum_heads(parts, seqs):
    size = lax.axis_size("tensor")
    split = parts.reshape(parts.shape[0], seqs, 2, size, -1)
    other = swap_cores(split)
    chip = split + other[:, :, ::-1]
    total = chip
    for j in range(1, size):
        ahead = from_ahead(chip, j)
        total = total + jnp.roll(ahead, j, axis=3)
    return total.reshape(parts.shape)


def sum_gains(part):
    chip = part + swap_cores(part)
    total = chip
    for j in range(1, lax.axis_size("tensor")):
        total = total + from_ahead(chip, j)
    return total


def local_order(table, section_index, tensor_rank):
    seqs, length = table.shape
    size = lax.axis_size("tensor")
    split = table.reshape(seqs, size, 2, length // (2 * size))
    twice = jnp.concatenate([split, split], axis=1)
    turned = lax.dynamic_slice_in_dim(twice, tensor_rank, size, 1)
    turned = jnp.where(section_index == 0, turned, turned[:, :, ::-1])
    return jnp.transpose(turned, (0, 2, 1, 3)).reshape(seqs, length)


def doc_tables(seg_rows, section_index, tensor_rank):
    same_doc = seg_rows[:, :, None] == seg_rows[:, None, :]
    index_row = jnp.arange(seg_rows.shape[1], dtype=jnp.int32)
    earlier = index_row[None, :] < index_row[:, None]
    positions = jnp.sum((same_doc & earlier[None]).astype(jnp.int32), axis=-1)
    positions = local_order(positions, section_index, tensor_rank)
    segs = local_order(seg_rows, section_index, tensor_rank)
    order = local_order(
        jnp.broadcast_to(index_row[None], seg_rows.shape), section_index, tensor_rank
    )
    visible = (segs[:, :, None] == segs[:, None, :]) & (order[:, None, :] <= order[:, :, None])
    half_dim = HD // 2
    inverse_freq = THETA ** (-(jnp.arange(half_dim, dtype=jnp.float32) * (2.0 / HD)))
    angles = positions.astype(jnp.float32)[..., None] * inverse_freq
    return (visible, jnp.cos(angles), jnp.sin(angles))


def rotate(vectors, cosine, sine_part):
    half_dim = HD // 2
    front_half = vectors[..., :half_dim]
    back_half = vectors[..., half_dim:]
    cos_wide = cosine[:, :, None, :]
    sin_wide = sine_part[:, :, None, :]
    return jnp.concatenate(
        [
            front_half * cos_wide - back_half * sin_wide,
            back_half * cos_wide + front_half * sin_wide,
        ],
        axis=-1,
    )


def masked_scores(query_rot, key_rot, visible):
    scores = jnp.einsum(
        "bshe,bthe->bhst", query_rot, key_rot, preferred_element_type=jnp.float32
    ) * HD ** (-0.5)
    return jnp.where(visible[:, None], scores, -jnp.inf)


def log_norm(masked):
    row_max = jnp.max(masked, axis=-1, keepdims=True)
    return row_max + jnp.log(jnp.sum(jnp.exp(masked - row_max), axis=-1, keepdims=True))


class Layer:
    def __init__(self, w_qkv, w_out, w_gate_up, w_down, gains, head_slot):
        self.w_qkv = w_qkv
        self.w_out = w_out
        self.w_gate_up = w_gate_up
        self.w_down = w_down
        self.gains = gains
        width = w_out.shape[0]
        whole = local_blocks(gains)
        self.query_gain = lax.dynamic_slice_in_dim(whole[0], head_slot * width, width)
        self.key_gain = lax.dynamic_slice_in_dim(whole[1], head_slot * width, width)
        self.head_slot = head_slot

    def attend(self, layer_in, tables):
        visible, cosine, sine_part = tables
        full = gather_tokens(layer_in.astype(jnp.bfloat16))
        seqs, slots, rows, _ = full.shape
        length = slots * rows
        tokens = seqs * length
        full = full.reshape(tokens, D)
        width = self.w_out.shape[0]
        heads = width // HD
        qkv = matmul(full, self.w_qkv)
        queries = qkv[:, :width]
        key_vecs = qkv[:, width : 2 * width]
        values = qkv[:, 2 * width :].astype(jnp.bfloat16).reshape(seqs, length, heads, HD)
        squares = sum_heads(
            jnp.stack([jnp.sum(queries * queries, axis=-1), jnp.sum(key_vecs * key_vecs, axis=-1)]),
            seqs,
        )
        scales = lax.rsqrt(squares / D + EPS)
        query_scale = scales[0][:, None]
        key_scale = scales[1][:, None]
        query_hat = queries * query_scale
        key_hat = key_vecs * key_scale
        query_rot = rotate(
            (query_hat * self.query_gain).reshape(seqs, length, heads, HD), cosine, sine_part
        ).astype(jnp.bfloat16)
        key_rot = rotate(
            (key_hat * self.key_gain).reshape(seqs, length, heads, HD), cosine, sine_part
        ).astype(jnp.bfloat16)
        masked = masked_scores(query_rot, key_rot, visible)
        log_total = log_norm(masked)
        probs = jnp.exp(masked - log_total)
        mix = jnp.einsum(
            "bhst,bthe->bshe",
            probs.astype(jnp.bfloat16),
            values,
            preferred_element_type=jnp.float32,
        )
        mix = mix.astype(jnp.bfloat16).reshape(tokens, width)
        attn = scatter_tokens(matmul(mix, self.w_out).reshape(seqs, slots, rows, D))
        attn_scale = rms_scale(attn)
        attn_hat = attn * attn_scale
        hidden = layer_in + attn_hat * self.gains[2]
        kept = dict(
            full=full,
            query_hat=query_hat,
            key_hat=key_hat,
            query_scale=query_scale,
            key_scale=key_scale,
            query_rot=query_rot,
            key_rot=key_rot,
            values=values,
            log_total=log_total,
            mix=mix,
            attn_hat=attn_hat,
            attn_scale=attn_scale,
            tables=tables,
        )
        return hidden, kept

    def feed(self, hidden, kept):
        full = gather_tokens(hidden.astype(jnp.bfloat16))
        seqs, slots, rows, _ = full.shape
        full = full.reshape(seqs * slots * rows, D)
        units = self.w_down.shape[0]
        gate_up = matmul(full, self.w_gate_up)
        gate = gate_up[:, :units]
        up = gate_up[:, units:]
        swiglu = (jax.nn.silu(gate) * up).astype(jnp.bfloat16)
        ffn = scatter_tokens(matmul(swiglu, self.w_down).reshape(seqs, slots, rows, D))
        ffn_scale = rms_scale(ffn)
        ffn_hat = ffn * ffn_scale
        output = hidden + ffn_hat * self.gains[3]
        kept = dict(
            kept,
            full_hidden=full,
            gate=gate,
            up=up,
            swiglu=swiglu,
            ffn_hat=ffn_hat,
            ffn_scale=ffn_scale,
        )
        return output, kept

    def feed_back(self, back_output, kept):
        ffn_hat = kept["ffn_hat"]
        gain_ffn = jnp.sum(back_output * ffn_hat, axis=(0, 1))
        back_hat = back_output * self.gains[3]
        back_ffn = kept["ffn_scale"] * (
            back_hat - ffn_hat * jnp.mean(back_hat * ffn_hat, axis=-1, keepdims=True)
        )
        back_ffn, gain_ffn = lax.optimization_barrier((back_ffn.astype(jnp.bfloat16), gain_ffn))
        full = gather_tokens(back_ffn)
        shape = full.shape
        full = full.reshape(-1, D)
        grad_down = inner_left(kept["swiglu"], full)
        back_swiglu = inner_right(full, self.w_down)
        gate = kept["gate"]
        up = kept["up"]
        sigmoid_gate = jax.nn.sigmoid(gate)
        back_gate = back_swiglu * up * sigmoid_gate * (1.0 + gate * (1.0 - sigmoid_gate))
        back_up = back_swiglu * jax.nn.silu(gate)
        back_gate_up = jnp.concatenate([back_gate, back_up], axis=1).astype(jnp.bfloat16)
        back_hidden = back_output + scatter_tokens(
            inner_right(back_gate_up, self.w_gate_up).reshape(shape)
        )
        grad_gate_up = inner_left(kept["full_hidden"], back_gate_up)
        return back_hidden, dict(down=grad_down, gate_up=grad_gate_up, gain_ffn=gain_ffn)

    def attend_back(self, back_hidden, kept):
        visible, cosine, sine_part = kept["tables"]
        attn_hat = kept["attn_hat"]
        gain_attn = jnp.sum(back_hidden * attn_hat, axis=(0, 1))
        back_hat = back_hidden * self.gains[2]
        back_attn = kept["attn_scale"] * (
            back_hat - attn_hat * jnp.mean(back_hat * attn_hat, axis=-1, keepdims=True)
        )
        back_attn, gain_attn = lax.optimization_barrier(
            (back_attn.astype(jnp.bfloat16), gain_attn)
        )
        full = gather_tokens(back_attn)
        shape = full.shape
        full = full.reshape(-1, D)
        tokens = full.shape[0]
        query_rot = kept["query_rot"]
        key_rot = kept["key_rot"]
        values = kept["values"]
        heads_shape = values.shape
        grad_out = inner_left(kept["mix"], full)
        back_mix = inner_right(full, self.w_out).astype(jnp.bfloat16).reshape(heads_shape)
        masked = masked_scores(query_rot, key_rot, visible)
        probs = jnp.exp(masked - kept["log_total"])
        back_values = jnp.einsum(
            "bhst,bshe->bthe",
            probs.astype(jnp.bfloat16),
            back_mix,
            preferred_element_type=jnp.float32,
        ).astype(jnp.bfloat16)
        back_probs = jnp.einsum(
            "bshe,bthe->bhst", back_mix, values, preferred_element_type=jnp.float32
        )
        row_dot = jnp.sum(probs * back_probs, axis=-1, keepdims=True)
        back_scores = (probs * (back_probs - row_dot) * HD ** (-0.5)).astype(jnp.bfloat16)
        back_query_rot = jnp.einsum(
            "bhst,bthe->bshe", back_scores, key_rot, preferred_element_type=jnp.float32
        )
        back_key_rot = jnp.einsum(
            "bhst,bshe->bthe", back_scores, query_rot, preferred_element_type=jnp.float32
        )
        width = self.w_out.shape[0]
        back_query_gained = rotate(back_query_rot, cosine, -sine_part).reshape(tokens, width)
        back_key_gained = rotate(back_key_rot, cosine, -sine_part).reshape(tokens, width)
        query_hat = kept["query_hat"]
        key_hat = kept["key_hat"]
        gain_query = jnp.sum(back_query_gained * query_hat, axis=0)
        gain_key = jnp.sum(back_key_gained * key_hat, axis=0)
        back_query_hat = back_query_gained * self.query_gain
        back_key_hat = back_key_gained * self.key_gain
        dots = sum_heads(
            jnp.stack(
                [
                    jnp.sum(back_query_hat * query_hat, axis=-1),
                    jnp.sum(back_key_hat * key_hat, axis=-1),
                ]
            ),
            shape[0],
        )
        back_query = kept["query_scale"] * (back_query_hat - query_hat * (dots[0] / D)[:, None])
        back_key = kept["key_scale"] * (back_key_hat - key_hat * (dots[1] / D)[:, None])
        back_qkv = jnp.concatenate(
            [
                back_query.astype(jnp.bfloat16),
                back_key.astype(jnp.bfloat16),
                back_values.reshape(tokens, width),
            ],
            axis=1,
        )
        back_input = back_hidden + scatter_tokens(inner_right(back_qkv, self.w_qkv).reshape(shape))
        grad_qkv = inner_left(kept["full"], back_qkv)
        zero_width = jnp.zeros((2, D), jnp.float32)
        start = self.head_slot * width
        gain_heads = local_blocks(
            lax.dynamic_update_slice(zero_width, jnp.stack([gain_query, gain_key]), (0, start))
        )
        gain_part = jnp.concatenate([gain_heads, gain_attn[None]], axis=0)
        return back_input, dict(out=grad_out, qkv=grad_qkv, gains=gain_part)


def whole_step(boundary, segments, w_qkv, w_out, w_gate_up, w_down, gains):
    section_index = lax.axis_index("section")
    tensor_rank = lax.axis_index("tensor")
    first = section_index == 0

    def shared(block, axis):
        half = block.shape[axis] // 2
        kept = lax.dynamic_slice_in_dim(block, section_index * half, half, axis)
        sent = lax.dynamic_slice_in_dim(block, (1 - section_index) * half, half, axis)
        received = swap_cores(sent)
        return jnp.where(first, kept, received), jnp.where(first, received, kept)

    rows_in, rows_back = [local_blocks(rows) for rows in shared(boundary[0], 1)]
    model = w_qkv.shape[1]
    qkv_halves = [half.reshape(model, -1) for half in shared(w_qkv[0], 2)]
    out_halves = shared(w_out[0], 0)
    gate_up_halves = [half.reshape(model, -1) for half in shared(w_gate_up[0], 2)]
    down_halves = shared(w_down[0], 0)
    other_gains = swap_cores(gains[0])
    both_gains = jnp.concatenate(
        [jnp.where(first, gains[0], other_gains), jnp.where(first, other_gains, gains[0])], axis=0
    )
    all_gains = jnp.concatenate(gather_blocks(both_gains), axis=1)
    head_slot = tensor_rank * 2 + section_index
    layers = []
    for index in range(2):
        layers.append(
            Layer(
                jnp.concatenate(gather_blocks(qkv_halves[index]), axis=0),
                jnp.concatenate(gather_blocks(out_halves[index]), axis=1),
                jnp.concatenate(gather_blocks(gate_up_halves[index]), axis=0),
                jnp.concatenate(gather_blocks(down_halves[index]), axis=1),
                all_gains[4 * index : 4 * index + 4],
                head_slot,
            )
        )
    tables = doc_tables(segments, section_index, tensor_rank)
    state = rows_in
    kept = []
    outs = []
    for layer in layers:
        hidden, now = layer.attend(state, tables)
        state, now = layer.feed(hidden, now)
        kept.append(now)
        outs.append(state)
    state = rows_back
    backs = [None, None]
    all_grads = [None, None]
    width = w_out.shape[1] // 2
    for index in (1, 0):
        hidden, feed_grads = layers[index].feed_back(state, kept[index])
        down = scatter_blocks(split_last(feed_grads["down"]))
        gate_up = scatter_blocks(split_first(feed_grads["gate_up"]))
        state, grads = layers[index].attend_back(hidden, kept[index])
        backs[index] = state
        qkv = scatter_blocks(split_first(grads["qkv"]))
        gain_part = jnp.concatenate([grads["gains"], feed_grads["gain_ffn"][None]], axis=0)
        if index == 1:
            state, gain_part = lax.optimization_barrier((state, gain_part))
        gain_rows = sum_gains(gain_part)
        out = scatter_blocks(
            split_last(
                jnp.concatenate([grads["out"], jnp.pad(gain_rows, ((0, 28), (0, 0)))], axis=0)
            ),
        )
        all_grads[index] = dict(
            down=down.astype(jnp.bfloat16),
            gate_up=gate_up.astype(jnp.bfloat16),
            qkv=qkv.astype(jnp.bfloat16),
            out=out[:width].astype(jnp.bfloat16),
            gains=out[width : width + 4],
        )
    first_grads, second_grads = all_grads

    def collected(name, axis, shape):
        mine_first = first_grads[name].reshape(shape)
        mine_second = second_grads[name].reshape(shape)
        to_second = one_way(mine_second, 0)
        to_first = one_way(mine_first, 1)
        low = jnp.where(first, mine_first, to_second)
        high = jnp.where(first, to_first, mine_second)
        return jnp.concatenate([low, high], axis=axis).astype(jnp.float32)[None]

    def placed(first_rows, second_rows):
        to_second = one_way(second_rows, 0)
        to_first = one_way(first_rows, 1)
        low = jnp.where(first, first_rows, to_second)
        high = jnp.where(first, to_first, second_rows)
        return local_blocks(jnp.concatenate([low, high], axis=1))[None]

    units = w_down.shape[1] // 2
    return (
        placed(outs[0], outs[1]),
        placed(backs[0], backs[1]),
        collected("qkv", 2, (model, 3, width)),
        collected("out", 0, (width, w_out.shape[2])),
        collected("gate_up", 2, (model, 2, units)),
        collected("down", 0, (units, w_down.shape[2])),
        jnp.where(first, first_grads["gains"], second_grads["gains"])[None],
    )


def solution(mesh):
    return jax.shard_map(
        whole_step,
        mesh=mesh,
        in_specs=(
            P("section", "dp", "tensor", None),
            P("dp", None),
            P("section", "dp", None, "tensor"),
            P("section", "tensor", "dp"),
            P("section", "dp", None, "tensor"),
            P("section", "tensor", "dp"),
            P("section", None, "dp"),
        ),
        out_specs=(
            P("section", "dp", "tensor", None),
            P("section", "dp", "tensor", None),
            P("section", "dp", None, "tensor"),
            P("section", "tensor", "dp"),
            P("section", "dp", None, "tensor"),
            P("section", "tensor", "dp"),
            P("section", None, "dp"),
        ),
        check_vma=False,
    )
```

```python
import jax
import jax.numpy as jnp
from jax import lax
from jax.experimental import pallas as pl
from jax.experimental.pallas import tpu as pltpu
from jax.sharding import PartitionSpec as P


D = 2048
HD = 128


EPS = 1e-06
THETA = 500000.0
HIDDEN = -1e30


def matmul(left, right):
    return jnp.dot(left, right, preferred_element_type=jnp.float32)


def inner_left(left, right):
    return lax.dot_general(
        left, right, (((0,), (0,)), ((), ())), preferred_element_type=jnp.float32
    )


def inner_right(left, right):
    return lax.dot_general(
        left, right, (((1,), (1,)), ((), ())), preferred_element_type=jnp.float32
    )


def rms_scale(vectors):
    return lax.rsqrt(jnp.mean(vectors * vectors, axis=-1, keepdims=True) + EPS)


def swap_cores(block):
    return lax.ppermute(block, "section", [(0, 1), (1, 0)])


def one_way(block, source):
    return lax.ppermute(block, "section", [(source, 1 - source)])


def from_ahead(block, distance):
    size = lax.axis_size("tensor")
    return lax.ppermute(block, "tensor", [(i, (i - distance) % size) for i in range(size)])


def to_ahead(block, distance):
    size = lax.axis_size("tensor")
    return lax.ppermute(block, "tensor", [(i, (i + distance) % size) for i in range(size)])


def square():
    return lax.axis_size("dp") == 4


def across(block, flip):
    return lax.ppermute(block, "dp", [(i, i ^ flip) for i in range(4)])


def local_blocks(array):
    if not square():
        return array
    rank = lax.axis_index("dp")
    width = array.shape[-1] // 4
    return jnp.concatenate(
        [
            lax.dynamic_slice_in_dim(array, (rank ^ j) * width, width, array.ndim - 1)
            for j in range(4)
        ],
        axis=-1,
    )


def gather_blocks(block):
    if not square():
        return list(lax.all_gather(block, "dp", axis=0, tiled=False))
    half = block.shape[0] // 2
    by_x = across(block, 1)
    by_y = across(block, 2)
    low = across(by_y[:half], 1)
    high = across(by_x[half:], 2)
    return [block, by_x, by_y, jnp.concatenate([low, high], axis=0)]


def scatter_blocks(blocks):
    wire = jnp.bfloat16
    if not square():
        whole = jnp.concatenate([block.astype(wire) for block in blocks], axis=0)
        return lax.psum_scatter(whole, "dp", scatter_dimension=0, tiled=True).astype(jnp.float32)
    half = blocks[0].shape[0] // 2
    own, to_x, to_y, to_far = [block.astype(wire) for block in blocks]
    by_x = across(jnp.concatenate([to_far[:half], to_x[:half]], axis=0), 1)
    by_y = across(jnp.concatenate([to_far[half:], to_y[half:]], axis=0), 2)

    def added(left, right):
        return left.astype(jnp.float32) + right.astype(jnp.float32)

    high = across(added(to_x[half:], by_y[:half]).astype(wire), 1)
    low = across(added(to_y[:half], by_x[:half]).astype(wire), 2)
    by_x, by_y, low, high = lax.optimization_barrier((by_x, by_y, low, high))
    low = added(own[:half], by_x[half:]) + low.astype(jnp.float32)
    high = added(own[half:], by_y[half:]) + high.astype(jnp.float32)
    return jnp.concatenate([low, high], axis=0)


def split_last(array):
    return jnp.split(array, lax.axis_size("dp"), axis=-1)


def split_first(array):
    return jnp.split(array, lax.axis_size("dp"), axis=0)


def gather_tokens(rows):
    size = lax.axis_size("tensor")
    slots = [rows]
    for j in range(1, size):
        slots.append(from_ahead(rows, j))
    mine = jnp.stack(slots, axis=1)
    other = swap_cores(mine)
    return jnp.concatenate([mine, other], axis=1)


def scatter_tokens(partial):
    size = lax.axis_size("tensor")
    other = swap_cores(partial[:, size:].astype(jnp.bfloat16))
    chip = partial[:, :size] + other.astype(jnp.float32)
    total = chip[:, 0]
    sent = chip.astype(jnp.bfloat16)
    for j in range(1, size):
        total = total + to_ahead(sent[:, j], j).astype(jnp.float32)
    return total


def head_parts(parts, seqs):
    size = lax.axis_size("tensor")
    other = swap_cores(parts)
    turned_over = other.reshape(8, seqs, 2, -1)[:, :, ::-1].reshape(parts.shape)
    chip = parts + turned_over
    ahead = []
    for j in range(1, size):
        ahead.append(from_ahead(chip, j))
    return [chip] + ahead


def sum_gains(part):
    chip = part + swap_cores(part)
    total = chip
    for j in range(1, lax.axis_size("tensor")):
        total = total + from_ahead(chip, j)
    return total


def local_order(table, section_index, tensor_rank):
    seqs, length = table.shape
    size = lax.axis_size("tensor")
    split = table.reshape(seqs, size, 2, length // (2 * size))
    twice = jnp.concatenate([split, split], axis=1)
    turned = lax.dynamic_slice_in_dim(twice, tensor_rank, size, 1)
    turned = jnp.where(section_index == 0, turned, turned[:, :, ::-1])
    return jnp.transpose(turned, (0, 2, 1, 3)).reshape(seqs, length)


def doc_tables(seg_rows, section_index, tensor_rank):
    same_doc = seg_rows[:, :, None] == seg_rows[:, None, :]
    index_row = jnp.arange(seg_rows.shape[1], dtype=jnp.int32)
    earlier = index_row[None, :] < index_row[:, None]
    positions = jnp.sum((same_doc & earlier[None]).astype(jnp.int32), axis=-1)
    positions = local_order(positions, section_index, tensor_rank)
    segs = local_order(seg_rows, section_index, tensor_rank)
    order = local_order(
        jnp.broadcast_to(index_row[None], seg_rows.shape), section_index, tensor_rank
    )
    visible = (segs[:, :, None] == segs[:, None, :]) & (order[:, None, :] <= order[:, :, None])
    half_dim = HD // 2
    inverse_freq = THETA ** (-(jnp.arange(half_dim, dtype=jnp.float32) * (2.0 / HD)))
    angles = positions.astype(jnp.float32)[..., None] * inverse_freq
    cosine = jnp.cos(angles)
    sine = jnp.sin(angles)
    return (
        jnp.where(visible, 0.0, HIDDEN),
        jnp.concatenate([cosine, cosine], axis=-1),
        jnp.concatenate([-sine, sine], axis=-1),
    )


def exact_dot(left, right, contract):
    return lax.dot_general(
        left,
        right,
        (contract, ((), ())),
        precision=lax.Precision.HIGHEST,
        preferred_element_type=jnp.float32,
    )


def token_sums(products):
    shape = (8, products.shape[1])
    row = lax.broadcasted_iota(jnp.int32, shape, 0)
    col = lax.broadcasted_iota(jnp.int32, shape, 1)
    low = (row == 0) & (col < shape[1] // 2)
    high = (row == 1) & (col >= shape[1] // 2)
    picks = jnp.where(low | high, 1.0, 0.0)
    return exact_dot(picks, products, ((1,), (1,)))


def column(values, row, width):
    picks = lax.broadcasted_iota(jnp.int32, (8, width), 0) == row
    return exact_dot(values, jnp.where(picks, 1.0, 0.0), ((0,), (0,)))


def aligned_sum(refs):
    tokens = refs[0].shape[1]
    half = tokens // 2
    turn = half // len(refs)
    parts = []
    for low in (0, half):
        total = refs[0][:, low : low + half]
        for j in range(1, len(refs)):
            total = total + pltpu.roll(refs[j][:, low : low + half], turn * j, 1)
        parts.append(total)
    return jnp.concatenate(parts, axis=1)


def turned(vectors, cosine, sine, sign):
    return vectors * cosine + sign * (pltpu.roll(vectors, HD // 2, 1) * sine)


def head_probs(query_rot, key_rot, bias):
    scores = lax.dot_general(
        query_rot, key_rot, (((1,), (1,)), ((), ())), preferred_element_type=jnp.float32
    )
    scores = scores * HD ** (-0.5) + bias
    raised = jnp.exp(scores - jnp.max(scores, axis=1, keepdims=True))
    return raised / jnp.sum(raised, axis=1, keepdims=True)


def squares_kernel(qkv_ref, out_ref):
    width = qkv_ref.shape[1] // 3
    pair = qkv_ref[:, : 2 * width]
    out_ref[...] = token_sums(pair * pair)


def attend_kernel(*refs):
    qkv_ref, gain_ref, bias_ref, cos_ref, sin_ref = refs[:5]
    parts, (mix_ref, total_ref) = refs[5:-2], refs[-2:]
    width = qkv_ref.shape[1] // 3
    total = aligned_sum(parts)
    total_ref[...] = total
    scales = lax.rsqrt(total / D + EPS)
    query_scale = column(scales, 0, HD)
    key_scale = column(scales, 1, HD)
    bias, cosine, sine = bias_ref[0], cos_ref[0], sin_ref[0]
    for low in range(0, width, HD):
        cols = slice(low, low + HD)
        keys = slice(width + low, width + low + HD)
        query_rot = turned(
            qkv_ref[:, cols] * query_scale * gain_ref[0:1, cols], cosine, sine, 1.0
        ).astype(jnp.bfloat16)
        key_rot = turned(
            qkv_ref[:, keys] * key_scale * gain_ref[1:2, cols], cosine, sine, 1.0
        ).astype(jnp.bfloat16)
        probs = head_probs(query_rot, key_rot, bias)
        values = qkv_ref[:, 2 * width + low : 2 * width + low + HD].astype(jnp.bfloat16)
        mix_ref[:, cols] = matmul(probs.astype(jnp.bfloat16), values).astype(jnp.bfloat16)


def attend_back_kernel(
    full_ref,
    w_out_ref,
    qkv_ref,
    total_ref,
    gain_ref,
    bias_ref,
    cos_ref,
    sin_ref,
    back_ref,
    values_ref,
    dots_ref,
    gains_ref,
    prod_ref,
):
    width = qkv_ref.shape[1] // 3

    @pl.when(pl.program_id(0) == 0)
    def _():
        gains_ref[...] = jnp.zeros_like(gains_ref)

    back_mix = inner_right(full_ref[...], w_out_ref[...]).astype(jnp.bfloat16)
    scales = lax.rsqrt(total_ref[...] / D + EPS)
    query_scale = column(scales, 0, HD)
    key_scale = column(scales, 1, HD)
    bias, cosine, sine = bias_ref[0], cos_ref[0], sin_ref[0]
    for low in range(0, width, HD):
        cols = slice(low, low + HD)
        keys = slice(width + low, width + low + HD)
        query_hat = qkv_ref[:, cols] * query_scale
        key_hat = qkv_ref[:, keys] * key_scale
        query_gain = gain_ref[0:1, cols]
        key_gain = gain_ref[1:2, cols]
        query_rot = turned(query_hat * query_gain, cosine, sine, 1.0).astype(jnp.bfloat16)
        key_rot = turned(key_hat * key_gain, cosine, sine, 1.0).astype(jnp.bfloat16)
        probs = head_probs(query_rot, key_rot, bias)
        values = qkv_ref[:, 2 * width + low : 2 * width + low + HD].astype(jnp.bfloat16)
        back = back_mix[:, cols]
        values_ref[:, cols] = inner_left(probs.astype(jnp.bfloat16), back).astype(jnp.bfloat16)
        back_probs = inner_right(back, values)
        row_dot = jnp.sum(probs * back_probs, axis=1, keepdims=True)
        back_scores = (probs * (back_probs - row_dot) * HD ** (-0.5)).astype(jnp.bfloat16)
        back_query = turned(matmul(back_scores, key_rot), cosine, sine, -1.0)
        back_key = turned(inner_left(back_scores, query_rot), cosine, sine, -1.0)
        gains_ref[0:1, cols] += jnp.sum(back_query * query_hat, axis=0, keepdims=True)
        gains_ref[1:2, cols] += jnp.sum(back_key * key_hat, axis=0, keepdims=True)
        back_query = back_query * query_gain
        back_key = back_key * key_gain
        back_ref[:, cols] = back_query
        back_ref[:, keys] = back_key
        prod_ref[:, cols] = back_query * query_hat
        prod_ref[:, keys] = back_key * key_hat
    dots_ref[...] = token_sums(prod_ref[...])


def settle_kernel(*refs):
    qkv_ref, total_ref, back_ref, values_ref = refs[:4]
    parts, out_ref = refs[4:-1], refs[-1]
    width = qkv_ref.shape[1] // 3
    means = aligned_sum(parts) / D
    scales = lax.rsqrt(total_ref[...] / D + EPS)
    for row, low in ((0, 0), (1, width)):
        cols = slice(low, low + width)
        scale = column(scales, row, width)
        hat = qkv_ref[:, cols] * scale
        out_ref[:, cols] = (scale * (back_ref[:, cols] - hat * column(means, row, width))).astype(
            jnp.bfloat16
        )
    out_ref[:, 2 * width :] = values_ref[...]


def by_sequence(kernel, seqs, operands, results, scratch=(), flops=0):
    def spec(shape, which):
        block = list(shape)
        if which is None:
            return pl.BlockSpec(shape, lambda s: (0,) * len(shape))
        if which == "table":
            block[0] = 1
            return pl.BlockSpec(tuple(block), lambda s: (s,) + (0,) * (len(shape) - 1))
        block[which] //= seqs
        if which == 0:
            return pl.BlockSpec(tuple(block), lambda s: (s, 0))
        return pl.BlockSpec(tuple(block), lambda s: (0, s))

    moved = sum(array.size * array.dtype.itemsize for array, _ in operands)
    return pl.pallas_call(
        kernel,
        grid=(seqs,),
        in_specs=[spec(array.shape, which) for array, which in operands],
        out_specs=[spec(shape, which) for shape, _, which in results],
        out_shape=[jax.ShapeDtypeStruct(shape, dtype) for shape, dtype, _ in results],
        scratch_shapes=list(scratch),
        cost_estimate=pl.CostEstimate(flops=flops, bytes_accessed=moved, transcendentals=0),
    )(*[array for array, _ in operands])


class Layer:
    def __init__(self, w_qkv, w_out, w_gate_up, w_down, gains, head_slot):
        self.w_qkv = w_qkv
        self.w_out = w_out
        self.w_gate_up = w_gate_up
        self.w_down = w_down
        self.gains = gains
        width = w_out.shape[0]
        whole = local_blocks(gains)
        self.head_gains = lax.dynamic_slice_in_dim(whole, head_slot * width, width, 1).astype(
            jnp.float32
        )
        self.head_slot = head_slot

    def attend(self, layer_in, tables):
        full = gather_tokens(layer_in.astype(jnp.bfloat16))
        seqs, slots, rows, _ = full.shape
        length = slots * rows
        tokens = seqs * length
        full = full.reshape(tokens, D)
        width = self.w_out.shape[0]
        qkv = matmul(full, self.w_qkv)
        bias, cosine, sine = tables
        (squares,) = by_sequence(
            squares_kernel,
            seqs,
            [(qkv, 0)],
            [((8, tokens), jnp.float32, 1)],
            flops=tokens * width * 64,
        )
        parts = head_parts(squares, seqs)
        mix, total = by_sequence(
            attend_kernel,
            seqs,
            [(qkv, 0), (self.head_gains, None)]
            + [(table, "table") for table in (bias, cosine, sine)]
            + [(part, 1) for part in parts],
            [((tokens, width), jnp.bfloat16, 0), ((8, tokens), jnp.float32, 1)],
            flops=tokens * length * width * 4,
        )
        attn = scatter_tokens(matmul(mix, self.w_out).reshape(seqs, slots, rows, D))
        attn_scale = rms_scale(attn)
        attn_hat = attn * attn_scale
        hidden = layer_in + attn_hat * self.gains[2]
        kept = dict(
            full=full,
            qkv=qkv,
            total=total,
            mix=mix,
            attn_hat=attn_hat,
            attn_scale=attn_scale,
            tables=tables,
        )
        return hidden, kept

    def feed(self, hidden, kept):
        full = gather_tokens(hidden.astype(jnp.bfloat16))
        seqs, slots, rows, _ = full.shape
        full = full.reshape(seqs * slots * rows, D)
        units = self.w_down.shape[0]
        gate_up = matmul(full, self.w_gate_up)
        gate = gate_up[:, :units]
        up = gate_up[:, units:]
        swiglu = (jax.nn.silu(gate) * up).astype(jnp.bfloat16)
        ffn = scatter_tokens(matmul(swiglu, self.w_down).reshape(seqs, slots, rows, D))
        ffn_scale = rms_scale(ffn)
        ffn_hat = ffn * ffn_scale
        output = hidden + ffn_hat * self.gains[3]
        kept = dict(
            kept,
            full_hidden=full,
            gate=gate,
            up=up,
            swiglu=swiglu,
            ffn_hat=ffn_hat,
            ffn_scale=ffn_scale,
        )
        return output, kept

    def feed_back(self, back_output, kept):
        ffn_hat = kept["ffn_hat"]
        gain_ffn = jnp.sum(back_output * ffn_hat, axis=(0, 1))
        back_hat = back_output * self.gains[3]
        back_ffn = kept["ffn_scale"] * (
            back_hat - ffn_hat * jnp.mean(back_hat * ffn_hat, axis=-1, keepdims=True)
        )
        back_ffn, gain_ffn = lax.optimization_barrier((back_ffn.astype(jnp.bfloat16), gain_ffn))
        full = gather_tokens(back_ffn)
        shape = full.shape
        full = full.reshape(-1, D)
        grad_down = inner_left(kept["swiglu"], full)
        back_swiglu = inner_right(full, self.w_down)
        gate = kept["gate"]
        up = kept["up"]
        sigmoid_gate = jax.nn.sigmoid(gate)
        back_gate = back_swiglu * up * sigmoid_gate * (1.0 + gate * (1.0 - sigmoid_gate))
        back_up = back_swiglu * jax.nn.silu(gate)
        back_gate_up = jnp.concatenate([back_gate, back_up], axis=1).astype(jnp.bfloat16)
        back_hidden = back_output + scatter_tokens(
            inner_right(back_gate_up, self.w_gate_up).reshape(shape)
        )
        grad_gate_up = inner_left(kept["full_hidden"], back_gate_up)
        return back_hidden, dict(down=grad_down, gate_up=grad_gate_up, gain_ffn=gain_ffn)

    def attend_back(self, back_hidden, kept):
        attn_hat = kept["attn_hat"]
        gain_attn = jnp.sum(back_hidden * attn_hat, axis=(0, 1))
        back_hat = back_hidden * self.gains[2]
        back_attn = kept["attn_scale"] * (
            back_hat - attn_hat * jnp.mean(back_hat * attn_hat, axis=-1, keepdims=True)
        )
        back_attn, gain_attn = lax.optimization_barrier(
            (back_attn.astype(jnp.bfloat16), gain_attn)
        )
        full = gather_tokens(back_attn)
        shape = full.shape
        full = full.reshape(-1, D)
        tokens = full.shape[0]
        width = self.w_out.shape[0]
        bias, cosine, sine = kept["tables"]
        seqs, length = bias.shape[:2]
        qkv, total = kept["qkv"], kept["total"]
        back, back_values, dots, gain_heads = by_sequence(
            attend_back_kernel,
            seqs,
            [(full, 0), (self.w_out, None), (qkv, 0), (total, 1), (self.head_gains, None)]
            + [(table, "table") for table in (bias, cosine, sine)],
            [
                ((tokens, 2 * width), jnp.float32, 0),
                ((tokens, width), jnp.bfloat16, 0),
                ((8, tokens), jnp.float32, 1),
                ((8, width), jnp.float32, None),
            ],
            scratch=[pltpu.VMEM((length, 2 * width), jnp.float32)],
            flops=tokens * width * (2 * D + length * 10),
        )
        parts = head_parts(dots, seqs)
        (back_qkv,) = by_sequence(
            settle_kernel,
            seqs,
            [(qkv, 0), (total, 1), (back, 0), (back_values, 0)] + [(part, 1) for part in parts],
            [((tokens, 3 * width), jnp.bfloat16, 0)],
            flops=tokens * width * 64,
        )
        grad_out = inner_left(kept["mix"], full)
        back_input = back_hidden + scatter_tokens(inner_right(back_qkv, self.w_qkv).reshape(shape))
        grad_qkv = inner_left(kept["full"], back_qkv)
        zero_width = jnp.zeros((2, D), jnp.float32)
        start = self.head_slot * width
        gain_heads = local_blocks(
            lax.dynamic_update_slice(zero_width, gain_heads[:2], (0, start))
        )
        gain_part = jnp.concatenate([gain_heads, gain_attn[None]], axis=0)
        return back_input, dict(out=grad_out, qkv=grad_qkv, gains=gain_part)


def whole_step(boundary, segments, w_qkv, w_out, w_gate_up, w_down, gains):
    section_index = lax.axis_index("section")
    tensor_rank = lax.axis_index("tensor")
    first = section_index == 0

    def shared(block, axis):
        half = block.shape[axis] // 2
        kept = lax.dynamic_slice_in_dim(block, section_index * half, half, axis)
        sent = lax.dynamic_slice_in_dim(block, (1 - section_index) * half, half, axis)
        received = swap_cores(sent)
        return jnp.where(first, kept, received), jnp.where(first, received, kept)

    rows_in, rows_back = [local_blocks(rows) for rows in shared(boundary[0], 1)]
    model = w_qkv.shape[1]
    qkv_halves = [half.reshape(model, -1) for half in shared(w_qkv[0], 2)]
    out_halves = shared(w_out[0], 0)
    gate_up_halves = [half.reshape(model, -1) for half in shared(w_gate_up[0], 2)]
    down_halves = shared(w_down[0], 0)
    other_gains = swap_cores(gains[0])
    both_gains = jnp.concatenate(
        [jnp.where(first, gains[0], other_gains), jnp.where(first, other_gains, gains[0])], axis=0
    )
    all_gains = jnp.concatenate(gather_blocks(both_gains), axis=1)
    head_slot = tensor_rank * 2 + section_index
    layers = []
    for index in range(2):
        layers.append(
            Layer(
                jnp.concatenate(gather_blocks(qkv_halves[index]), axis=0),
                jnp.concatenate(gather_blocks(out_halves[index]), axis=1),
                jnp.concatenate(gather_blocks(gate_up_halves[index]), axis=0),
                jnp.concatenate(gather_blocks(down_halves[index]), axis=1),
                all_gains[4 * index : 4 * index + 4],
                head_slot,
            )
        )
    tables = doc_tables(segments, section_index, tensor_rank)
    state = rows_in
    kept = []
    outs = []
    for layer in layers:
        hidden, now = layer.attend(state, tables)
        state, now = layer.feed(hidden, now)
        kept.append(now)
        outs.append(state)
    state = rows_back
    backs = [None, None]
    all_grads = [None, None]
    width = w_out.shape[1] // 2
    for index in (1, 0):
        hidden, feed_grads = layers[index].feed_back(state, kept[index])
        down = scatter_blocks(split_last(feed_grads["down"]))
        gate_up = scatter_blocks(split_first(feed_grads["gate_up"]))
        state, grads = layers[index].attend_back(hidden, kept[index])
        backs[index] = state
        qkv = scatter_blocks(split_first(grads["qkv"]))
        gain_part = jnp.concatenate([grads["gains"], feed_grads["gain_ffn"][None]], axis=0)
        if index == 1:
            state, gain_part = lax.optimization_barrier((state, gain_part))
        gain_rows = sum_gains(gain_part)
        out = scatter_blocks(
            split_last(
                jnp.concatenate([grads["out"], jnp.pad(gain_rows, ((0, 28), (0, 0)))], axis=0)
            ),
        )
        all_grads[index] = dict(
            down=down.astype(jnp.bfloat16),
            gate_up=gate_up.astype(jnp.bfloat16),
            qkv=qkv.astype(jnp.bfloat16),
            out=out[:width].astype(jnp.bfloat16),
            gains=out[width : width + 4],
        )
    first_grads, second_grads = all_grads

    def collected(name, axis, shape):
        mine_first = first_grads[name].reshape(shape)
        mine_second = second_grads[name].reshape(shape)
        to_second = one_way(mine_second, 0)
        to_first = one_way(mine_first, 1)
        low = jnp.where(first, mine_first, to_second)
        high = jnp.where(first, to_first, mine_second)
        return jnp.concatenate([low, high], axis=axis).astype(jnp.float32)[None]

    def placed(first_rows, second_rows):
        to_second = one_way(second_rows, 0)
        to_first = one_way(first_rows, 1)
        low = jnp.where(first, first_rows, to_second)
        high = jnp.where(first, to_first, second_rows)
        return local_blocks(jnp.concatenate([low, high], axis=1))[None]

    units = w_down.shape[1] // 2
    return (
        placed(outs[0], outs[1]),
        placed(backs[0], backs[1]),
        collected("qkv", 2, (model, 3, width)),
        collected("out", 0, (width, w_out.shape[2])),
        collected("gate_up", 2, (model, 2, units)),
        collected("down", 0, (units, w_down.shape[2])),
        jnp.where(first, first_grads["gains"], second_grads["gains"])[None],
    )


def solution(mesh):
    return jax.shard_map(
        whole_step,
        mesh=mesh,
        in_specs=(
            P("section", "dp", "tensor", None),
            P("dp", None),
            P("section", "dp", None, "tensor"),
            P("section", "tensor", "dp"),
            P("section", "dp", None, "tensor"),
            P("section", "tensor", "dp"),
            P("section", None, "dp"),
        ),
        out_specs=(
            P("section", "dp", "tensor", None),
            P("section", "dp", "tensor", None),
            P("section", "dp", None, "tensor"),
            P("section", "tensor", "dp"),
            P("section", "dp", None, "tensor"),
            P("section", "tensor", "dp"),
            P("section", None, "dp"),
        ),
        check_vma=False,
    )
```
